32 devices in a mesh: groups: 2 (over x), seq: 16 (over z, y, core).
Axes of the slice: x: 2, y: 2, z: 4, core: 2. Of those that a mesh axis runs over, the one named last changes fastest.
Arguments:
- queries: bfloat16 [32, 384, 1280], P(('groups', 'seq')), parts along dimension 0, may hold values from -11 to 11
- key_vectors: bfloat16 [32, 384, 1280], P(('groups', 'seq')), parts along dimension 0, may hold values from -11 to 11
- value_vectors: bfloat16 [32, 384, 1280], P(('groups', 'seq')), parts along dimension 0, may hold values from -5 to 5
- out_grad: bfloat16 [32, 384, 1280], P(('groups', 'seq')), parts along dimension 0, may hold values from -5 to 5
- tile_lists: int32 [16, 5], P('groups'), parts along dimension 0, may hold values from -1 to 7, as said below
Outputs:
- attended: bfloat16 [32, 384, 1280], P(('groups', 'seq')), parts along dimension 0
- query_grad: bfloat16 [32, 384, 1280], P(('groups', 'seq')), parts along dimension 0
- key_grad: bfloat16 [32, 384, 1280], P(('groups', 'seq')), parts along dimension 0
- value_grad: bfloat16 [32, 384, 1280], P(('groups', 'seq')), parts along dimension 0
The draws below stay inside these ranges and needn't reach their ends.
There are 2 independent parts, one for each index of `groups`. The reference program is written for one: setup_inputs(seed, part) draws one part's arguments, and reference() takes and returns one part's arrays. A program takes and returns all parts, laid end to end along the dimension named above; each array names one. Nothing has to cross between parts.
Inputs may be any that keep to these rules, and one draw needn't show every extreme that they name: `tile_lists`: row s lists in ascending order tile s itself, every neighbour of s along the width inside the grid, and some of its neighbours along height and time, then -1 in the unused slots.
All inputs are finite; a program needn't handle non-finite values.
Results may differ from the reference program's by a relative error of at most 0.023.
Values may be sent and summed in bfloat16 or wider, within the bound.
A program may use at most 192 MiB of HBM per device.

```python
import jax
import jax.numpy as jnp
from jax import lax

HEADS = 20
HD = 128
TOK = 384
TILES = 8
ROWS = 16
HALF_W = 1280


def drawn_pair(key):
    shape = (ROWS, TOK, HEADS // 2 * HD)
    query_key, key_key = jax.random.split(jax.random.fold_in(key, 7), 2)
    query_draw = 1.4 * jax.random.truncated_normal(query_key, -4.0, 4.0, shape, jnp.float32)
    key_draw = 1.4 * jax.random.truncated_normal(key_key, -4.0, 4.0, shape, jnp.float32)
    return (query_draw, key_draw)


def draw_queries(key, part):
    return drawn_pair(key)[0].astype(jnp.bfloat16)


def draw_key_vectors(key, part):
    return drawn_pair(key)[1].astype(jnp.bfloat16)


def draw_tile_lists(key, part):
    grid_w = TILES // 4
    tile_slot = jnp.arange(TILES, dtype=jnp.int32)
    column = tile_slot // 4
    tile_ids = jnp.stack([tile_slot, tile_slot - 4, tile_slot + 4, jnp.bitwise_xor(tile_slot, 1), jnp.bitwise_xor(tile_slot, 2)], axis=1)
    inside = jnp.stack([tile_slot >= 0, column > 0, column < grid_w - 1, tile_slot >= 0, tile_slot >= 0], axis=1)
    keeping = jax.random.randint(jax.random.fold_in(key, 3), (TILES, 5), 0, 4) > 0
    keeping = keeping.at[:, 0].set(True)
    keeping = keeping.at[:, 1].set(True)
    keeping = keeping.at[:, 2].set(True)
    entries = jnp.where(inside & keeping, tile_ids, TILES)
    entries = jnp.sort(entries, axis=1)
    return jnp.where(entries >= TILES, -1, entries).astype(jnp.int32)


def block_scale(key, dims, cuts, low, high):
    level, own = 1.0, jax.random.fold_in(key, 6)
    for dim, parts in cuts:
        heights = jnp.exp(jax.random.uniform(jax.random.fold_in(own, dim), (parts,), jnp.float32, low / len(cuts), high / len(cuts)))
        level = level * jnp.repeat(heights, dims[dim] // parts).reshape([-1 if axis == dim else 1 for axis in range(len(dims))])
    return level


def gaussian(key, shape, spread, bound, pieces=(), held_as=jnp.bfloat16):
    result = spread * jax.random.normal(key, shape, jnp.float32)
    if pieces:
        result = result * block_scale(key, shape, pieces, -0.22, 0.18)
    return jnp.clip(result, -bound, bound).astype(held_as)


def setup_inputs(seed: int = 0, part: int = 0) -> dict:
    streams_of = jax.random.split(jax.random.key(seed), 6)
    part_keys = jax.random.split(jax.random.fold_in(streams_of[5], part), 6)
    queries = draw_queries(jax.random.fold_in(jax.random.fold_in(streams_of[5], part), 71), part)
    key_vectors = draw_key_vectors(jax.random.fold_in(jax.random.fold_in(streams_of[5], part), 71), part)
    value_vectors = gaussian(part_keys[2], (ROWS, TOK, HALF_W), 2.0, 5.0, ((0, 16),))
    out_grad = gaussian(part_keys[3], (ROWS, TOK, HALF_W), 1.0, 5.0, ((0, 16),))
    tile_lists = draw_tile_lists(jax.random.fold_in(jax.random.fold_in(streams_of[5], part), 71), part)
    return dict(queries=queries, key_vectors=key_vectors, value_vectors=value_vectors, out_grad=out_grad, tile_lists=tile_lists)


def neighbour_tiles(tile_slot):
    grid_w = TILES // 4
    column = tile_slot // 4
    tile_ids = jnp.stack([tile_slot, tile_slot - 4, tile_slot + 4, jnp.bitwise_xor(tile_slot, 1), jnp.bitwise_xor(tile_slot, 2)]).astype(jnp.int32)
    inside = jnp.stack([column >= 0, column > 0, column < grid_w - 1, column >= 0, column >= 0])
    return jnp.clip(tile_ids, 0, TILES - 1).astype(jnp.int32), inside


def reference(queries, key_vectors, value_vectors, out_grad, tile_lists):
    score_scale = HD ** -0.5
    head_count = HEADS // 2

    def shaped(rows):
        return rows.astype(jnp.float32).reshape(rows.shape[:-1] + (head_count, HD))

    def query_pass(row_index):
        tile_slot = row_index // 2
        half_index = row_index % 2
        tile_ids, inside = neighbour_tiles(tile_slot)
        listed = tile_lists[tile_slot]
        in_use = inside & jnp.any(listed[None, :] == tile_ids[:, None], axis=1)
        key_index = (2 * tile_ids + half_index).astype(jnp.int32)
        query_row = shaped(queries[row_index])
        grad_row = shaped(out_grad[row_index])
        near_keys = shaped(key_vectors[key_index])
        near_values = shaped(value_vectors[key_index])
        scores = jnp.einsum("qhd,ckhd->hqck", query_row, near_keys) * score_scale
        scores = jnp.where(in_use[None, None, :, None], scores, -jnp.inf)
        row_top = jnp.max(scores, axis=(2, 3))
        log_total = row_top + jnp.log(jnp.sum(jnp.exp(scores - row_top[:, :, None, None]), axis=(2, 3)))
        chance = jnp.exp(scores - log_total[:, :, None, None])
        rounded = lax.optimization_barrier(chance.astype(jnp.bfloat16)).astype(jnp.float32)
        attended = jnp.einsum("hqck,ckhd->qhd", rounded, near_values).reshape(TOK, HALF_W).astype(jnp.bfloat16)
        attended_wide = lax.optimization_barrier(attended).astype(jnp.float32).reshape(TOK, head_count, HD)
        delta_rows = jnp.sum(grad_row * attended_wide, axis=2).T
        pressure = jnp.einsum("qhd,ckhd->hqck", grad_row, near_values)
        score_grad = lax.optimization_barrier((chance * (pressure - delta_rows[:, :, None, None])).astype(jnp.bfloat16)).astype(jnp.float32)
        query_grad = (score_scale * jnp.einsum("hqck,ckhd->qhd", score_grad, near_keys)).reshape(TOK, HALF_W).astype(jnp.bfloat16)
        return attended, query_grad, log_total, delta_rows

    attended, query_grad, log_totals, delta_all = lax.map(query_pass, jnp.arange(ROWS, dtype=jnp.int32))

    def key_pass(row_index):
        tile_slot = row_index // 2
        half_index = row_index % 2
        tile_ids, inside = neighbour_tiles(tile_slot)
        their_lists = tile_lists[tile_ids]
        in_use = inside & jnp.any(their_lists == tile_slot, axis=1)
        query_index = (2 * tile_ids + half_index).astype(jnp.int32)
        near_queries = shaped(queries[query_index])
        near_grads = shaped(out_grad[query_index])
        near_totals = log_totals[query_index]
        near_deltas = delta_all[query_index]
        own_keys = shaped(key_vectors[row_index])
        own_values = shaped(value_vectors[row_index])
        scores = jnp.einsum("cqhd,khd->chqk", near_queries, own_keys) * score_scale
        scores = jnp.where(in_use[:, None, None, None], scores, -jnp.inf)
        chance = jnp.exp(scores - near_totals[:, :, :, None])
        rounded = lax.optimization_barrier(chance.astype(jnp.bfloat16)).astype(jnp.float32)
        pressure = jnp.einsum("cqhd,khd->chqk", near_grads, own_values)
        score_grad = lax.optimization_barrier((chance * (pressure - near_deltas[:, :, :, None])).astype(jnp.bfloat16)).astype(jnp.float32)
        value_terms = lax.optimization_barrier(jnp.einsum("chqk,cqhd->ckhd", rounded, near_grads).astype(jnp.bfloat16)).astype(jnp.float32)
        key_terms = lax.optimization_barrier((score_scale * jnp.einsum("chqk,cqhd->ckhd", score_grad, near_queries)).astype(jnp.bfloat16)).astype(jnp.float32)
        key_grad = jnp.sum(key_terms, axis=0).reshape(TOK, HALF_W).astype(jnp.bfloat16)
        value_grad = jnp.sum(value_terms, axis=0).reshape(TOK, HALF_W).astype(jnp.bfloat16)
        return key_grad, value_grad

    key_grad, value_grad = lax.map(key_pass, jnp.arange(ROWS, dtype=jnp.int32))
    return attended, query_grad, key_grad, value_grad
```

```python
import math

import jax
import jax.numpy as jnp
from jax import lax
from jax.experimental import pallas as pl
from jax.experimental.pallas import tpu as pltpu
from jax.sharding import PartitionSpec as P

HD = 128
SCALE = HD ** (-0.5)
LOG2E = math.log2(math.e)
VMEM_LIMIT = 60_000_000

NT = (((1,), (1,)), ((), ()))
NN = (((1,), (0,)), ((), ()))


def dot(a, b, dims):
    return lax.dot_general(a, b, dims, preferred_element_type=jnp.float32)


def query_kernel(count, flags, q_ref, g_ref, *refs):
    k_refs, v_refs = refs[:count], refs[count : 2 * count]
    out_ref, dq_ref, stat_ref = refs[2 * count :]
    q, g = q_ref[...], g_ref[...]
    scores = []
    for b in range(count):
        s = dot(q, k_refs[b][...], NT) * (SCALE * LOG2E)
        scores.append(s if b == 0 else jnp.where(flags[b] != 0, s, -jnp.inf))
    top = jnp.max(scores[0], axis=1, keepdims=True)
    for s in scores[1:]:
        top = jnp.maximum(top, jnp.max(s, axis=1, keepdims=True))
    powers = [jnp.exp2(s - top) for s in scores]
    total = sum(jnp.sum(p, axis=1, keepdims=True) for p in powers)
    inverse = 1.0 / total
    chances = [p * inverse for p in powers]
    mixed = sum(dot(c.astype(jnp.bfloat16), v[...], NN) for c, v in zip(chances, v_refs))
    attended = mixed.astype(jnp.bfloat16)
    out_ref[...] = attended
    delta = jnp.sum(
        g.astype(jnp.float32) * attended.astype(jnp.float32), axis=1, keepdims=True
    )
    dq = None
    for c, k, v in zip(chances, k_refs, v_refs):
        ds = (c * (dot(g, v[...], NT) - delta)).astype(jnp.bfloat16)
        term = dot(ds, k[...], NN)
        dq = term if dq is None else dq + term
    dq_ref[...] = (dq * SCALE).astype(jnp.bfloat16)
    log_total = top + jnp.log2(total)
    lane = lax.broadcasted_iota(jnp.int32, (q.shape[0], HD), 1)
    packed = jnp.where(lane == 0, log_total, delta)
    stat_ref[0] = packed.T[:8]


def key_kernel(count, flags, k_ref, v_ref, *refs):
    q_refs, g_refs, stat_refs = refs[:count], refs[count : 2 * count], refs[2 * count : 3 * count]
    dk_ref, dv_ref = refs[3 * count :]
    k, v = k_ref[...], v_ref[...]
    dk = dv = None
    for b in range(count):
        q, g = q_refs[b][...], g_refs[b][...]
        log_total, delta = stat_refs[b][0, 0:1, :], stat_refs[b][0, 1:2, :]
        p = jnp.exp2(dot(k, q, NT) * (SCALE * LOG2E) - log_total)
        if b:
            p = jnp.where(flags[b] != 0, p, 0.0)
        v_term = dot(p.astype(jnp.bfloat16), g, NN)
        ds = (p * (dot(v, g, NT) - delta)).astype(jnp.bfloat16)
        k_term = dot(ds, q, NN)
        dk, dv = (k_term, v_term) if b == 0 else (dk + k_term, dv + v_term)
    dk_ref[...] = (dk * SCALE).astype(jnp.bfloat16)
    dv_ref[...] = dv.astype(jnp.bfloat16)


def specs(tok):
    head = pl.BlockSpec((tok, HD), lambda h: (0, h))
    stat = pl.BlockSpec((1, 8, tok), lambda h: (h, 0, 0))
    return head, stat, pl.BlockSpec(memory_space=pltpu.SMEM)


def cost(tok, width, count, dots):
    return pl.CostEstimate(
        flops=2 * dots * count * tok * tok * width,
        bytes_accessed=2 * (2 * count + 4) * tok * width,
        transcendentals=count * tok * tok * width // HD,
    )


def query_side(flags, q, g, keys, values):
    tok, width = q.shape
    heads, count = width // HD, len(keys)
    head, stat, smem = specs(tok)
    rows = jax.ShapeDtypeStruct((tok, width), jnp.bfloat16)
    return pl.pallas_call(
        lambda *refs: query_kernel(count, *refs),
        grid=(heads,),
        in_specs=[smem] + [head] * (2 + 2 * count),
        out_specs=[head, head, stat],
        out_shape=[rows, rows, jax.ShapeDtypeStruct((heads, 8, tok), jnp.float32)],
        compiler_params=pltpu.CompilerParams(vmem_limit_bytes=VMEM_LIMIT),
        cost_estimate=cost(tok, width, count, 4),
        name="query_side",
    )(flags, q, g, *keys, *values)


def key_side(flags, k, v, queries, grads, stats):
    tok, width = k.shape
    heads, count = width // HD, len(queries)
    head, stat, smem = specs(tok)
    rows = jax.ShapeDtypeStruct((tok, width), jnp.bfloat16)
    return pl.pallas_call(
        lambda *refs: key_kernel(count, *refs),
        grid=(heads,),
        in_specs=[smem] + [head] * (2 + 2 * count) + [stat] * count,
        out_specs=[head, head],
        out_shape=[rows, rows],
        compiler_params=pltpu.CompilerParams(vmem_limit_bytes=VMEM_LIMIT),
        cost_estimate=cost(tok, width, count, 4),
        name="key_side",
    )(flags, k, v, *queries, *grads, *stats)


def on_device(queries, key_vectors, value_vectors, out_grad, tile_lists):
    q, k, v, g = queries[0], key_vectors[0], value_vectors[0], out_grad[0]
    size = lax.axis_size("seq")
    grid_w = size // 8
    slot = lax.axis_index("seq") // 2
    column = slot // 4

    def flip(bit):
        return [(i, i ^ bit) for i in range(size)]

    def shift(step):
        return [(i, i + step) for i in range(size) if 0 <= i + step < size]

    true = jnp.bool_(True)
    if grid_w == 2:
        near = [(flip(8), slot ^ 4, true)]
    else:
        near = [
            (shift(8), slot - 4, column > 0),
            (shift(-8), slot + 4, column < grid_w - 1),
        ]
    near += [(flip(4), slot ^ 2, true), (flip(2), slot ^ 1, true)]

    def attends(tile, target):
        listed = lax.dynamic_index_in_dim(tile_lists, tile, 0, keepdims=False)
        return jnp.any(listed == target)

    reads, read_by = [true], [true]
    for _, tile, inside in near:
        safe = jnp.clip(tile, 0, tile_lists.shape[0] - 1)
        reads.append(inside & attends(slot, tile))
        read_by.append(inside & attends(safe, slot))
    reads = jnp.stack(reads).astype(jnp.int32)
    read_by = jnp.stack(read_by).astype(jnp.int32)

    def gather(value):
        return [value] + [lax.ppermute(value, "seq", route) for route, _, _ in near]

    keys, values = gather(k), gather(v)
    all_q, all_g = gather(q), gather(g)
    attended, query_grad, stat = query_side(reads, q, g, keys, values)
    key_grad, value_grad = key_side(read_by, k, v, all_q, all_g, gather(stat))
    return attended[None], query_grad[None], key_grad[None], value_grad[None]


def solution(mesh):
    rows = P(("groups", "seq"), None, None)
    return jax.shard_map(
        on_device,
        mesh=mesh,
        in_specs=(rows, rows, rows, rows, P("groups", None)),
        out_specs=(rows, rows, rows, rows),
        check_vma=False,
    )
```
